32 devices in a mesh: gx: 8 (over z, x), gy: 2 (over y), pa: 2 (over core).
Axes of the slice: x: 2, y: 2, z: 4, core: 2. Of those that a mesh axis runs over, the one named last changes fastest.
Arguments:
- leaf_maps: bfloat16 [8, 2, 2, 1024, 1024], P('gx', 'gy', None, 'pa'), may hold values from -0.125 to 0.125
- face_index: int32 [8, 2, 1024], P('gx', 'gy'), may hold values from 0 to 1023, each once within a row
- order_x: int32 [4, 2], replicated, may hold values from 0 to 1
- order_y: int32 [4, 1], replicated, may hold values from 0 to 1
- traces: float32 [8, 2, 2, 1024], P('gx', 'gy'), may hold values from -6 to 6
Outputs:
- merged_map: bfloat16 [8, 2, 2, 2, 128, 1024], P('gx', 'gy', 'pa')
- outgoing: float32 [8, 2, 2, 2, 128], P('gx', 'gy', 'pa')
The draws below stay inside these ranges and needn't reach their ends.
Inputs may be any that keep to these rules, and one draw needn't show every extreme that they name: `face_index`: each row is a permutation of 0 to 1023.
All inputs are finite; a program needn't handle non-finite values.
Results may differ from the reference program's by a relative error of at most 0.0058.
Values may be sent and summed in bfloat16 or wider, within the bound.
A program may use at most 64 MiB of HBM per device.

```python
import jax
import jax.numpy as jnp
from jax import lax

ORDER = 2048
FC = 1024
NGX = 8
NGY = 2
NBX = 4
NBY = 1
NPA = 2
RW = 128


def plant(entries, stream_key, low, high):
    longest = entries.shape.index(max(entries.shape))
    spots = []
    for shift in (0, 1):
        where = [jax.random.randint(jax.random.fold_in(stream_key, axis), (), 0, length) for axis, length in enumerate(entries.shape)]
        where[longest] = (where[longest] + shift) % entries.shape[longest]
        spots.append(tuple(where))
    return entries.at[spots[0]].set(low).at[spots[1]].set(high)


def shard_levels(own_key, dims, pieces, low, largest):
    level = 1.0
    for position, parts in pieces:
        steps = jax.random.uniform(jax.random.fold_in(jax.random.fold_in(own_key, 6), position), (parts,), jnp.float32, low / len(pieces), largest / len(pieces))
        level = level * jnp.repeat(jnp.exp(steps), dims[position] // parts).reshape((-1,) + (1,) * (len(dims) - 1 - position))
    return level


def noise(stream_key, dims, spread, limit, split=(), held_as=jnp.bfloat16):
    factor_of = shard_levels(stream_key, dims, split, -0.22, 0.18) if split else 1.0
    values = jax.random.normal(stream_key, dims, jnp.float32) * spread * factor_of
    return jnp.minimum(jnp.maximum(values, -limit), limit).astype(held_as)


def setup_inputs(seed: int = 0) -> dict:
    key_of = jax.random.split(jax.random.key(seed), 6)
    return {
        "leaf_maps": noise(key_of[0], (NGX, NGY, 2, FC, FC), ORDER ** -0.5, 0.125, ((0, 8), (1, 2), (3, 2))),
        "face_index": jax.vmap(lambda own: jax.random.permutation(own, FC))(jax.random.split(key_of[1], NGX * NGY)).reshape((NGX, NGY, FC)).astype(jnp.int32),
        "order_x": plant(jax.random.randint(key_of[2], (NBX, NGY), 0, 2), jax.random.fold_in(key_of[2], 1), 0, 1).astype(jnp.int32),
        "order_y": plant(jax.random.randint(key_of[3], (NBX, NBY), 0, 2), jax.random.fold_in(key_of[3], 1), 0, 1).astype(jnp.int32),
        "traces": noise(key_of[4], (NGX, NGY, 2, FC), 1.0, 6.0, ((0, 8), (1, 2)), jnp.float32),
    }


def complex_product(left_panel, right_panel):
    real_part = jnp.dot(left_panel[0], right_panel[0], preferred_element_type=jnp.float32) - jnp.dot(left_panel[1], right_panel[1], preferred_element_type=jnp.float32)
    imag_part = jnp.dot(left_panel[0], right_panel[1], preferred_element_type=jnp.float32) + jnp.dot(left_panel[1], right_panel[0], preferred_element_type=jnp.float32)
    return jnp.stack([real_part, imag_part]).astype(jnp.bfloat16)


def product_pairs(left_stack, right_stack):
    return lax.map(lambda both: complex_product(both[0], both[1]), (left_stack, right_stack))


def reference(leaf_maps, face_index, order_x, order_y, traces):
    index_full = jnp.broadcast_to(face_index[:, :, None, None, :], leaf_maps.shape)
    leaves = jnp.take_along_axis(leaf_maps, index_full, axis=4)
    pairs = leaves.reshape(NBX, 2, NGY, 2, FC, FC)
    chosen = (order_x == 1)[:, :, None, None, None]
    right_one = jnp.where(chosen, pairs[:, 1], pairs[:, 0]).reshape(NBX * NGY, 2, FC, FC)
    left_one = jnp.where(chosen, pairs[:, 0], pairs[:, 1]).reshape(NBX * NGY, 2, FC, FC)
    merged_one = product_pairs(left_one, right_one).reshape(NBX, NBY, 2, 2, FC, FC)
    chosen_two = (order_y == 1)[:, :, None, None, None]
    right_two = jnp.where(chosen_two, merged_one[:, :, 1], merged_one[:, :, 0]).reshape(NBX * NBY, 2, FC, FC)
    left_two = jnp.where(chosen_two, merged_one[:, :, 0], merged_one[:, :, 1]).reshape(NBX * NBY, 2, FC, FC)
    merged_two = product_pairs(left_two, right_two).reshape(NBX, NBY, 2, FC, FC)
    incoming = traces.reshape(NBX, 2, NBY, 2, 2, FC).sum(axis=(1, 3))
    wide = merged_two.astype(jnp.float32)
    hp = lax.Precision.HIGHEST
    real_out = jnp.einsum("ijrc,ijc->ijr", wide[:, :, 0], incoming[:, :, 0], precision=hp) - jnp.einsum("ijrc,ijc->ijr", wide[:, :, 1], incoming[:, :, 1], precision=hp)
    imag_out = jnp.einsum("ijrc,ijc->ijr", wide[:, :, 0], incoming[:, :, 1], precision=hp) + jnp.einsum("ijrc,ijc->ijr", wide[:, :, 1], incoming[:, :, 0], precision=hp)
    box_out = jnp.stack([real_out, imag_out], axis=2)
    laid_map = merged_two.reshape(NBX, NBY, 2, NPA, 2, 2, RW, FC).transpose(0, 4, 1, 5, 3, 2, 6, 7).reshape(NGX, NGY, NPA, 2, RW, FC)
    laid_out = box_out.reshape(NBX, NBY, 2, NPA, 2, 2, RW).transpose(0, 4, 1, 5, 3, 2, 6).reshape(NGX, NGY, NPA, 2, RW)
    return laid_map, laid_out
```

```python
import functools

import jax
import jax.numpy as jnp
from jax import lax
from jax.experimental import pallas as pl
from jax.experimental.pallas import tpu as pltpu
from jax.sharding import PartitionSpec as P

MESH = pl.DeviceIdType.MESH
CHUNKS = 4


def one_hot(index_row, size):
    rows = lax.broadcasted_iota(jnp.int32, (size, index_row.shape[1]), 0)
    return (rows == index_row).astype(jnp.float32).astype(jnp.bfloat16)


def kernel(
    role_ref, leaf_ref, index_ref, trace_ref, map_ref, out_ref,
    held, index_all, trace_all, picks, work, local_sem,
    xs, xr, ys, yr, ps, pr, ss, sr,
):
    gx, gy, pa = lax.axis_index("gx"), lax.axis_index("gy"), lax.axis_index("pa")
    half, vert = gx % 2, gy % 2
    xpeer = {"gx": gx + 1 - 2 * half}
    ypeer = {"gy": gy + 1 - 2 * vert}
    dpeer = {"gx": gx + 1 - 2 * half, "gy": gy + 1 - 2 * vert}
    cpeer = {"pa": 1 - pa}
    panel, width = leaf_ref.shape[1], leaf_ref.shape[2]
    step = panel // CHUNKS

    barrier = pltpu.get_barrier_semaphore()
    for peer in (xpeer, ypeer, dpeer, cpeer):
        pl.semaphore_signal(barrier, inc=1, device_id=peer, device_id_type=MESH)
    pl.semaphore_wait(barrier, 4)

    def send(src, dst, ssem, rsem, peer):
        copy = pltpu.make_async_remote_copy(
            src_ref=src, dst_ref=dst, send_sem=ssem, recv_sem=rsem,
            device_id=peer, device_id_type=MESH,
        )
        copy.start()
        return copy

    def part(rel, k):
        return held.at[rel, pa, :, pl.ds(k * step, step), :]

    small = []
    for n, peer in ((1, xpeer), (2, ypeer), (3, dpeer)):
        small.append(send(index_ref, index_all.at[n], ss.at[0, n], sr.at[0, n], peer))
        small.append(send(trace_ref, trace_all.at[n], ss.at[1, n], sr.at[1, n], peer))
    xorder = list(range(CHUNKS))
    yorder = [(k + CHUNKS // 2) % CHUNKS for k in xorder]
    xcopy, ycopy = {}, {}
    for kx, ky in zip(xorder, yorder):
        xcopy[kx] = send(leaf_ref.at[:, pl.ds(kx * step, step), :], part(1, kx), xs.at[0, kx], xr.at[0, kx], xpeer)
        ycopy[ky] = send(leaf_ref.at[:, pl.ds(ky * step, step), :], part(2, ky), ys.at[0, ky], yr.at[0, ky], ypeer)
    own = pltpu.make_async_copy(leaf_ref, held.at[0, pa], local_sem)
    own.start()
    shared = [send(leaf_ref, held.at[0, pa], ps.at[0, 0], pr.at[0, 0], cpeer)]

    index_all[0] = index_ref[...]
    trace_all[0] = trace_ref[...]
    for copy in small:
        copy.wait_recv()
    for role in range(4):
        picks[role] = one_hot(index_all[role_ref[role]], width)

    def share(rel, k):
        shared.append(send(part(rel, k), part(rel, k), ps.at[rel, k], pr.at[rel, k], cpeer))

    xfwd, yfwd = {}, {}
    for kx, ky in zip(xorder, yorder):
        xcopy[kx].wait_recv()
        if kx < CHUNKS // 2:
            yfwd[kx] = send(part(1, kx), part(3, kx), ys.at[1, kx], yr.at[1, kx], ypeer)
        share(1, kx)
        ycopy[ky].wait_recv()
        if ky >= CHUNKS // 2:
            xfwd[ky] = send(part(2, ky), part(3, ky), xs.at[1, ky], xr.at[1, ky], xpeer)
        share(2, ky)
    for ky, kx in zip(yfwd, xfwd):
        yfwd[ky].wait_recv()
        share(3, ky)
        xfwd[kx].wait_recv()
        share(3, kx)
    own.wait()
    for copy in shared:
        copy.wait_recv()

    rows = map_ref.shape[1]
    first = pl.multiple_of(half * (2 * rows) + vert * rows, rows)
    lead = role_ref[0]
    work[0, :rows] = held[lead, pa, 0, pl.ds(first, rows), :]
    work[0, rows:] = held[lead, pa, 1, pl.ds(first, rows), :]

    def pick(src, dst, role):
        value = jnp.dot(work[src], picks[role], preferred_element_type=jnp.float32)
        work[dst] = value.astype(jnp.bfloat16)

    tile = 256

    def times(src, dst, role):
        which = role_ref[role]
        left = work[src]

        @pl.loop(0, width // tile)
        def _(n):
            cols = pl.ds(pl.multiple_of(n * tile, tile), tile)
            by = []
            for c in range(2):
                total = jnp.dot(left[:, :panel], held[which, 0, c, :, cols], preferred_element_type=jnp.float32)
                total += jnp.dot(left[:, panel:], held[which, 1, c, :, cols], preferred_element_type=jnp.float32)
                by.append(total)
            real = by[0][:rows] - by[1][rows:]
            imag = by[1][:rows] + by[0][rows:]
            work[dst, :rows, cols] = real.astype(jnp.bfloat16)
            work[dst, rows:, cols] = imag.astype(jnp.bfloat16)

    pick(0, 1, 0)
    times(1, 0, 1)
    pick(0, 1, 1)
    times(1, 0, 2)
    pick(0, 1, 2)
    times(1, 0, 3)
    pick(0, 1, 3)
    map_ref[0] = work[1, :rows]
    map_ref[1] = work[1, rows:]
    trace = (trace_all[0] + trace_all[1]) + (trace_all[2] + trace_all[3])
    wide = work[1].astype(jnp.float32)
    dims = (((1,), (1,)), ((), ()))
    sums = lax.dot_general(trace, wide, dims, precision=lax.Precision.HIGHEST, preferred_element_type=jnp.float32)
    out_ref[0:1] = sums[0:1, :rows] - sums[1:2, rows:]
    out_ref[1:2] = sums[1:2, :rows] + sums[0:1, rows:]

    for copy in small + list(xcopy.values()) + list(ycopy.values()) + list(xfwd.values()) + list(yfwd.values()) + shared:
        copy.wait_send()


def per_device(leaf_maps, face_index, order_x, order_y, traces):
    leaf = leaf_maps[0, 0]
    _, panel, width = leaf.shape
    rows = panel // 4
    gx, gy = lax.axis_index("gx"), lax.axis_index("gy")
    half, vert = gx % 2, gy % 2
    base = gy // 2 * 2
    right2 = order_y[gx // 2, gy // 2]
    left2 = 1 - right2
    bit_left = order_x[gx // 2, base + left2]
    bit_right = order_x[gx // 2, base + right2]

    def rel(h, v):
        return (h ^ half) + 2 * (v ^ vert)

    roles = jnp.stack([
        rel(1 - bit_left, left2), rel(bit_left, left2),
        rel(1 - bit_right, right2), rel(bit_right, right2),
    ]).astype(jnp.int32)
    vmem = pl.BlockSpec(memory_space=pltpu.VMEM)
    dma = pltpu.SemaphoreType.DMA
    merged, outgoing = pl.pallas_call(
        kernel,
        out_shape=(
            jax.ShapeDtypeStruct((2, rows, width), jnp.bfloat16),
            jax.ShapeDtypeStruct((2, rows), jnp.float32),
        ),
        in_specs=[
            pl.BlockSpec(memory_space=pltpu.SMEM),
            pl.BlockSpec(memory_space=pl.ANY),
            vmem, vmem,
        ],
        out_specs=(vmem, vmem),
        scratch_shapes=[
            pltpu.VMEM((4, 2, 2, panel, width), jnp.bfloat16),
            pltpu.VMEM((4, 1, width), jnp.int32),
            pltpu.VMEM((4, 2, width), jnp.float32),
            pltpu.VMEM((4, width, width), jnp.bfloat16),
            pltpu.VMEM((2, 2 * rows, width), jnp.bfloat16),
            dma(()),
            dma((2, CHUNKS)), dma((2, CHUNKS)),
            dma((2, CHUNKS)), dma((2, CHUNKS)),
            dma((4, CHUNKS)), dma((4, CHUNKS)),
            dma((2, 4)), dma((2, 4)),
        ],
        compiler_params=pltpu.CompilerParams(
            collective_id=0, has_side_effects=True, vmem_limit_bytes=48 * 1024 * 1024
        ),
    )(roles, leaf, face_index[0], traces[0, 0])
    return (
        merged.reshape(1, 1, 1, 2, rows, width),
        outgoing.reshape(1, 1, 1, 2, rows),
    )


def solution(mesh):
    placed = (
        P("gx", "gy", None, "pa", None),
        P("gx", "gy", None),
        P(),
        P(),
        P("gx", "gy", None, None),
    )
    return jax.shard_map(
        per_device,
        mesh=mesh,
        in_specs=placed,
        out_specs=(P("gx", "gy", "pa", None, None, None), P("gx", "gy", "pa", None, None)),
        check_vma=False,
    )
```

```python
import jax
import jax.numpy as jnp
from jax import lax
from jax.experimental import pallas as pl
from jax.experimental.pallas import tpu as pltpu
from jax.sharding import PartitionSpec as P

MESH = pl.DeviceIdType.MESH
CHUNKS = 8
TILE = 256


def kernel(
    order_x_ref, order_y_ref, leaf_ref, index_ref, trace_ref, map_ref, out_ref,
    held, raw, index_own, pick, trace_all, work, local_sem,
    xs, xr, ys, yr, ps, pr, ss, sr,
):
    gx, gy, pa = lax.axis_index("gx"), lax.axis_index("gy"), lax.axis_index("pa")
    half, vert = gx % 2, gy % 2
    xpeer = {"gx": gx + 1 - 2 * half}
    ypeer = {"gy": gy + 1 - 2 * vert}
    dpeer = {"gx": gx + 1 - 2 * half, "gy": gy + 1 - 2 * vert}
    cpeer = {"pa": 1 - pa}
    panel, width = leaf_ref.shape[1], leaf_ref.shape[2]
    step = panel // CHUNKS
    rows = map_ref.shape[1]

    barrier = pltpu.get_barrier_semaphore()
    for peer in (xpeer, ypeer, dpeer, cpeer):
        pl.semaphore_signal(barrier, inc=1, device_id=peer, device_id_type=MESH)

    load_index = pltpu.make_async_copy(index_ref, index_own, local_sem.at[0])
    load_index.start()
    load_leaf = pltpu.make_async_copy(leaf_ref, raw, local_sem.at[1])
    load_leaf.start()
    load_trace = pltpu.make_async_copy(trace_ref, trace_all.at[0], local_sem.at[2])
    load_trace.start()

    def send(src, dst, ssem, rsem, peer):
        copy = pltpu.make_async_remote_copy(
            src_ref=src, dst_ref=dst, send_sem=ssem, recv_sem=rsem,
            device_id=peer, device_id_type=MESH,
        )
        copy.start()
        return copy

    def part(rel, k):
        return held.at[rel, :, pl.ds(pl.multiple_of(pa * panel + k * step, step), step), :]

    load_index.wait()
    index_row = index_own[...]
    grain = 256
    for n in range(width // grain):
        places = lax.broadcasted_iota(jnp.int32, (grain, width), 0) + n * grain
        pick[n * grain : (n + 1) * grain] = (places == index_row).astype(jnp.float32).astype(jnp.bfloat16)
    load_leaf.wait()

    def permute(k):
        chunk = raw[:, k * step : (k + 1) * step, :].reshape(2 * step, width)
        value = jnp.dot(chunk, pick[...], preferred_element_type=jnp.float32).astype(jnp.bfloat16)
        held[0, :, pl.ds(pl.multiple_of(pa * panel + k * step, step), step), :] = value.reshape(2, step, width)

    xorder = list(range(CHUNKS))
    yorder = [(k + CHUNKS // 2) % CHUNKS for k in xorder]
    xcopy, ycopy = {}, {}

    def send_x(k):
        xcopy[k] = send(part(0, k), part(1, k), xs.at[0, k], xr.at[0, k], xpeer)

    def send_y(k):
        ycopy[k] = send(part(0, k), part(2, k), ys.at[0, k], yr.at[0, k], ypeer)

    middle = CHUNKS // 2
    permute(0)
    permute(middle)
    pl.semaphore_wait(barrier, 4)
    for k in range(1, middle):
        send_x(k - 1)
        send_y(k - 1 + middle)
        permute(k)
        permute(k + middle)
    send_x(middle - 1)
    send_y(CHUNKS - 1)
    for k in range(middle):
        send_x(k + middle)
        send_y(k)
    own = held.at[0, :, pl.ds(pl.multiple_of(pa * panel, panel), panel), :]
    shared = [send(own, own, ps.at[0, 0], pr.at[0, 0], cpeer)]
    small = []
    for n, peer in ((1, xpeer), (2, ypeer), (3, dpeer)):
        small.append(send(trace_ref, trace_all.at[n], ss.at[n], sr.at[n], peer))

    def share(rel, k):
        shared.append(send(part(rel, k), part(rel, k), ps.at[rel, k], pr.at[rel, k], cpeer))

    xfwd, yfwd = {}, {}
    for kx, ky in zip(xorder, yorder):
        xcopy[kx].wait_recv()
        if kx < middle:
            yfwd[kx] = send(part(1, kx), part(3, kx), ys.at[1, kx], yr.at[1, kx], ypeer)
        share(1, kx)
        ycopy[ky].wait_recv()
        if ky >= middle:
            xfwd[ky] = send(part(2, ky), part(3, ky), xs.at[1, ky], xr.at[1, ky], xpeer)
        share(2, ky)
    for ky, kx in zip(yfwd, xfwd):
        yfwd[ky].wait_recv()
        share(3, ky)
        xfwd[kx].wait_recv()
        share(3, kx)
    load_trace.wait()
    for copy in small + shared:
        copy.wait_recv()

    pair, base = gx // 2, gy - vert
    right2 = order_y_ref[gy // 2, pair]
    left2 = 1 - right2
    bit_left = order_x_ref[base + left2, pair]
    bit_right = order_x_ref[base + right2, pair]

    def slot(h, v):
        return (h + half) % 2 + 2 * ((v + vert) % 2)

    first = pl.multiple_of(pa * panel + half * (2 * rows) + vert * rows, rows)
    lead = slot(1 - bit_left, left2)
    work[0, :rows] = held[lead, 0, pl.ds(first, rows), :]
    work[0, rows:] = held[lead, 1, pl.ds(first, rows), :]

    def times(src, dst, which):
        left = work[src]
        for n in range(width // TILE):
            cols = slice(n * TILE, (n + 1) * TILE)
            by = [jnp.dot(left, held[which, c, :, cols], preferred_element_type=jnp.float32) for c in range(2)]
            work[dst, :rows, cols] = (by[0][:rows] - by[1][rows:]).astype(jnp.bfloat16)
            work[dst, rows:, cols] = (by[1][:rows] + by[0][rows:]).astype(jnp.bfloat16)

    times(0, 1, slot(bit_left, left2))
    times(1, 0, slot(1 - bit_right, right2))
    times(0, 1, slot(bit_right, right2))
    map_ref[0] = work[1, :rows]
    map_ref[1] = work[1, rows:]
    trace = (trace_all[0] + trace_all[1]) + (trace_all[2] + trace_all[3])
    wide = work[1].astype(jnp.float32)
    ones = jnp.ones((8, 128), jnp.float32)
    dims = (((1,), (1,)), ((), ()))
    sums = []
    for c in range(2):
        scaled = wide * trace[c : c + 1]
        folded = scaled[:, :128]
        for n in range(1, width // 128):
            folded += scaled[:, n * 128 : (n + 1) * 128]
        sums.append(lax.dot_general(ones, folded, dims, precision=lax.Precision.HIGHEST, preferred_element_type=jnp.float32))
    out_ref[0:1] = sums[0][0:1, :rows] - sums[1][0:1, rows:]
    out_ref[1:2] = sums[1][0:1, :rows] + sums[0][0:1, rows:]

    for copy in small + list(xcopy.values()) + list(ycopy.values()) + list(xfwd.values()) + list(yfwd.values()) + shared:
        copy.wait_send()


def per_device(leaf_maps, face_index, order_x, order_y, traces):
    leaf = leaf_maps[0, 0]
    _, panel, width = leaf.shape
    rows = panel // 4
    vmem = pl.BlockSpec(memory_space=pltpu.VMEM)
    smem = pl.BlockSpec(memory_space=pltpu.SMEM)
    hbm = pl.BlockSpec(memory_space=pl.ANY)
    dma = pltpu.SemaphoreType.DMA
    merged, outgoing = pl.pallas_call(
        kernel,
        out_shape=(
            jax.ShapeDtypeStruct((2, rows, width), jnp.bfloat16),
            jax.ShapeDtypeStruct((2, rows), jnp.float32),
        ),
        in_specs=[smem, smem, hbm, hbm, hbm],
        out_specs=(vmem, vmem),
        scratch_shapes=[
            pltpu.VMEM((4, 2, 2 * panel, width), jnp.bfloat16),
            pltpu.VMEM((2, panel, width), jnp.bfloat16),
            pltpu.VMEM((1, width), jnp.int32),
            pltpu.VMEM((width, width), jnp.bfloat16),
            pltpu.VMEM((4, 2, width), jnp.float32),
            pltpu.VMEM((2, 2 * rows, width), jnp.bfloat16),
            dma((3,)),
            dma((2, CHUNKS)), dma((2, CHUNKS)),
            dma((2, CHUNKS)), dma((2, CHUNKS)),
            dma((4, CHUNKS)), dma((4, CHUNKS)),
            dma((4,)), dma((4,)),
        ],
        compiler_params=pltpu.CompilerParams(
            collective_id=0, has_side_effects=True, vmem_limit_bytes=67043328
        ),
    )(order_x.T, order_y.T, leaf, face_index[0], traces[0, 0])
    return (
        merged.reshape(1, 1, 1, 2, rows, width),
        outgoing.reshape(1, 1, 1, 2, rows),
    )


def solution(mesh):
    placed = (
        P("gx", "gy", None, "pa", None),
        P("gx", "gy", None),
        P(),
        P(),
        P("gx", "gy", None, None),
    )
    return jax.shard_map(
        per_device,
        mesh=mesh,
        in_specs=placed,
        out_specs=(P("gx", "gy", "pa", None, None, None), P("gx", "gy", "pa", None, None)),
        check_vma=False,
    )
```

```python
import jax
import jax.numpy as jnp
from jax import lax
from jax.experimental import pallas as pl
from jax.experimental.pallas import tpu as pltpu
from jax.sharding import PartitionSpec as P

MESH = pl.DeviceIdType.MESH
CHUNKS = 8
TILE = 256


def kernel(
    order_x_ref, order_y_ref, leaf_ref, index_ref, trace_ref, map_ref, out_ref,
    held, raw, index_own, pick, trace_all, work, ask, ask_in, reply, reply_in,
    local_sem,
    xs, xr, ys, yr, ps, pr, ss, sr,
):
    gx, gy, pa = lax.axis_index("gx"), lax.axis_index("gy"), lax.axis_index("pa")
    half, vert = gx % 2, gy % 2
    xpeer = {"gx": gx + 1 - 2 * half}
    ypeer = {"gy": gy + 1 - 2 * vert}
    dpeer = {"gx": gx + 1 - 2 * half, "gy": gy + 1 - 2 * vert}
    cpeer = {"pa": 1 - pa}
    panel, width = leaf_ref.shape[1], leaf_ref.shape[2]
    step = panel // CHUNKS
    rows = map_ref.shape[1]

    barrier = pltpu.get_barrier_semaphore()
    for peer in (xpeer, ypeer, dpeer, cpeer):
        pl.semaphore_signal(barrier, inc=1, device_id=peer, device_id_type=MESH)

    load_index = pltpu.make_async_copy(index_ref, index_own, local_sem.at[0])
    load_index.start()
    load_leaf = pltpu.make_async_copy(leaf_ref, raw, local_sem.at[1])
    load_leaf.start()
    load_trace = pltpu.make_async_copy(trace_ref, trace_all.at[0], local_sem.at[2])
    load_trace.start()

    def send(src, dst, ssem, rsem, peer):
        copy = pltpu.make_async_remote_copy(
            src_ref=src, dst_ref=dst, send_sem=ssem, recv_sem=rsem,
            device_id=peer, device_id_type=MESH,
        )
        copy.start()
        return copy

    def part(rel, k):
        return held.at[rel, :, pl.ds(pl.multiple_of(pa * panel + k * step, step), step), :]

    load_index.wait()
    index_row = index_own[...]
    grain = 256
    for n in range(width // grain):
        places = lax.broadcasted_iota(jnp.int32, (grain, width), 0) + n * grain
        pick[n * grain : (n + 1) * grain] = (places == index_row).astype(jnp.float32).astype(jnp.bfloat16)
    load_leaf.wait()

    def permute(k):
        chunk = raw[:, k * step : (k + 1) * step, :].reshape(2 * step, width)
        value = jnp.dot(chunk, pick[...], preferred_element_type=jnp.float32).astype(jnp.bfloat16)
        held[0, :, pl.ds(pl.multiple_of(pa * panel + k * step, step), step), :] = value.reshape(2, step, width)

    xcopy, ycopy = {}, {}

    def send_both(k):
        xcopy[k] = send(part(0, k), part(1, k), xs.at[k], xr.at[k], xpeer)
        ycopy[k] = send(part(0, k), part(2, k), ys.at[k], yr.at[k], ypeer)

    permute(0)
    permute(1)
    pl.semaphore_wait(barrier, 4)
    for k in range(2, CHUNKS):
        send_both(k - 2)
        permute(k)
    send_both(CHUNKS - 2)
    send_both(CHUNKS - 1)
    own = held.at[0, :, pl.ds(pl.multiple_of(pa * panel, panel), panel), :]
    shared = [send(own, own, ps.at[0, 0], pr.at[0, 0], cpeer)]
    small = []
    for n, peer in ((1, xpeer), (2, ypeer), (3, dpeer)):
        small.append(send(trace_ref, trace_all.at[n], ss.at[n], sr.at[n], peer))

    def share(rel, k):
        shared.append(send(part(rel, k), part(rel, k), ps.at[rel, k], pr.at[rel, k], cpeer))

    for k in range(CHUNKS):
        xcopy[k].wait_recv()
        share(1, k)
        ycopy[k].wait_recv()
        share(2, k)
    load_trace.wait()
    for copy in small + shared:
        copy.wait_recv()

    pair, base = gx // 2, gy - vert
    right2 = order_y_ref[gy // 2, pair]
    left2 = 1 - right2
    bit_left = order_x_ref[base + left2, pair]
    bit_right = order_x_ref[base + right2, pair]

    def slot(h, v):
        return (h + half) % 2 + 2 * ((v + vert) % 2)

    slots = [
        slot(1 - bit_left, left2), slot(bit_left, left2),
        slot(1 - bit_right, right2), slot(bit_right, right2),
    ]
    here = [jnp.minimum(which, 2) for which in slots]
    first = pl.multiple_of(pa * panel + half * (2 * rows) + vert * rows, rows)

    def times(src, dst, which, use=None):
        left = src[...].reshape(2 * rows, width)
        for n in range(width // TILE):
            cols = slice(n * TILE, (n + 1) * TILE)
            by = [jnp.dot(left, held[which, c, :, cols], preferred_element_type=jnp.float32) for c in range(2)]
            real = (by[0][:rows] - by[1][rows:]).astype(jnp.bfloat16)
            imag = (by[1][:rows] + by[0][rows:]).astype(jnp.bfloat16)
            if use is not None:
                real = jnp.where(use, real, src[0, :, cols])
                imag = jnp.where(use, imag, src[1, :, cols])
            dst[0, :, cols] = real
            dst[1, :, cols] = imag

    spot = lax.broadcasted_iota(jnp.int32, (rows, width), 0) + first
    unit = (lax.broadcasted_iota(jnp.int32, (rows, width), 1) == spot).astype(jnp.float32).astype(jnp.bfloat16)
    away = slots[0] == 3
    work[0, 0] = jnp.where(away, unit, held[here[0], 0, pl.ds(first, rows), :])
    work[0, 1] = jnp.where(away, jnp.zeros_like(unit), held[here[0], 1, pl.ds(first, rows), :])
    times(work.at[0], work.at[1], here[1], slots[2] // 3 + slots[3] // 3 > 0)
    times(work.at[1], ask, here[2], slots[3] == 3)
    peer = {"gx": gx + (1 - 2 * half) * (1 - pa), "gy": gy + (1 - 2 * vert) * pa}
    asked = send(ask, ask_in, ss.at[0], sr.at[0], peer)
    asked.wait_recv()
    times(ask_in, reply, 2 - pa)
    replied = send(reply, reply_in, ss.at[4], sr.at[4], peer)
    replied.wait_recv()
    times(reply_in, work.at[0], here[1], away)
    times(work.at[0], work.at[1], here[2], slots[0] // 3 + slots[1] // 3 > 0)
    times(work.at[1], map_ref, here[3], slots[3] != 3)
    trace = (trace_all[0] + trace_all[1]) + (trace_all[2] + trace_all[3])
    wide = map_ref[...].reshape(2 * rows, width).astype(jnp.float32)
    ones = jnp.ones((8, 128), jnp.float32)
    dims = (((1,), (1,)), ((), ()))
    sums = []
    for c in range(2):
        scaled = wide * trace[c : c + 1]
        folded = scaled[:, :128]
        for n in range(1, width // 128):
            folded += scaled[:, n * 128 : (n + 1) * 128]
        sums.append(lax.dot_general(ones, folded, dims, precision=lax.Precision.HIGHEST, preferred_element_type=jnp.float32))
    out_ref[0:1] = sums[0][0:1, :rows] - sums[1][0:1, rows:]
    out_ref[1:2] = sums[1][0:1, :rows] + sums[0][0:1, rows:]

    for copy in small + list(xcopy.values()) + list(ycopy.values()) + shared + [asked, replied]:
        copy.wait_send()


def per_device(leaf_maps, face_index, order_x, order_y, traces):
    leaf = leaf_maps[0, 0]
    _, panel, width = leaf.shape
    rows = panel // 4
    vmem = pl.BlockSpec(memory_space=pltpu.VMEM)
    smem = pl.BlockSpec(memory_space=pltpu.SMEM)
    hbm = pl.BlockSpec(memory_space=pl.ANY)
    dma = pltpu.SemaphoreType.DMA
    merged, outgoing = pl.pallas_call(
        kernel,
        out_shape=(
            jax.ShapeDtypeStruct((2, rows, width), jnp.bfloat16),
            jax.ShapeDtypeStruct((2, rows), jnp.float32),
        ),
        in_specs=[smem, smem, hbm, hbm, hbm],
        out_specs=(vmem, vmem),
        scratch_shapes=[
            pltpu.VMEM((3, 2, 2 * panel, width), jnp.bfloat16),
            pltpu.VMEM((2, panel, width), jnp.bfloat16),
            pltpu.VMEM((1, width), jnp.int32),
            pltpu.VMEM((width, width), jnp.bfloat16),
            pltpu.VMEM((4, 2, width), jnp.float32),
            pltpu.VMEM((2, 2, rows, width), jnp.bfloat16),
            pltpu.VMEM((2, rows, width), jnp.bfloat16),
            pltpu.VMEM((2, rows, width), jnp.bfloat16),
            pltpu.VMEM((2, rows, width), jnp.bfloat16),
            pltpu.VMEM((2, rows, width), jnp.bfloat16),
            dma((3,)),
            dma((CHUNKS,)), dma((CHUNKS,)),
            dma((CHUNKS,)), dma((CHUNKS,)),
            dma((3, CHUNKS)), dma((3, CHUNKS)),
            dma((5,)), dma((5,)),
        ],
        compiler_params=pltpu.CompilerParams(
            collective_id=0, has_side_effects=True, vmem_limit_bytes=67043328
        ),
    )(order_x.T, order_y.T, leaf, face_index[0], traces[0, 0])
    return (
        merged.reshape(1, 1, 1, 2, rows, width),
        outgoing.reshape(1, 1, 1, 2, rows),
    )


def solution(mesh):
    placed = (
        P("gx", "gy", None, "pa", None),
        P("gx", "gy", None),
        P(),
        P(),
        P("gx", "gy", None, None),
    )
    return jax.shard_map(
        per_device,
        mesh=mesh,
        in_specs=placed,
        out_specs=(P("gx", "gy", "pa", None, None, None), P("gx", "gy", "pa", None, None)),
        check_vma=False,
    )
```

```python
import jax
import jax.numpy as jnp
from jax import lax
from jax.experimental import pallas as pl
from jax.experimental.pallas import tpu as pltpu
from jax.sharding import PartitionSpec as P

MESH = pl.DeviceIdType.MESH
CHUNKS = 8
TILE = 256


def kernel(
    order_x_ref, order_y_ref, leaf_ref, index_ref, trace_ref, map_ref, out_ref,
    held, raw, index_own, pick, trace_all, work, ask, ask_in, reply, reply_in,
    total, local_sem,
    xs, xr, ys, yr, ps, pr, ss, sr, ts, tr,
):
    gx, gy, pa = lax.axis_index("gx"), lax.axis_index("gy"), lax.axis_index("pa")
    half, vert = gx % 2, gy % 2
    xpeer = {"gx": gx + 1 - 2 * half}
    ypeer = {"gy": gy + 1 - 2 * vert}
    dpeer = {"gx": gx + 1 - 2 * half, "gy": gy + 1 - 2 * vert}
    cpeer = {"pa": 1 - pa}
    panel, width = leaf_ref.shape[1], leaf_ref.shape[2]
    step = panel // CHUNKS
    rows = map_ref.shape[1]

    barrier = pltpu.get_barrier_semaphore()
    for peer in (xpeer, ypeer, dpeer, cpeer):
        pl.semaphore_signal(barrier, inc=1, device_id=peer, device_id_type=MESH)

    load_index = pltpu.make_async_copy(index_ref, index_own, local_sem.at[0])
    load_index.start()
    load_leaf = pltpu.make_async_copy(leaf_ref, raw, local_sem.at[1])
    load_leaf.start()
    load_trace = pltpu.make_async_copy(trace_ref, trace_all.at[0], local_sem.at[2])
    load_trace.start()

    def send(src, dst, ssem, rsem, peer):
        copy = pltpu.make_async_remote_copy(
            src_ref=src, dst_ref=dst, send_sem=ssem, recv_sem=rsem,
            device_id=peer, device_id_type=MESH,
        )
        copy.start()
        return copy

    def part(rel, k):
        return held.at[rel, :, pl.ds(pl.multiple_of(pa * panel + k * step, step), step), :]

    load_index.wait()
    index_row = index_own[...]
    grain = 256
    for n in range(width // grain):
        places = lax.broadcasted_iota(jnp.int32, (grain, width), 0) + n * grain
        pick[n * grain : (n + 1) * grain] = (places == index_row).astype(jnp.float32).astype(jnp.bfloat16)
    load_leaf.wait()

    def permute(k):
        chunk = raw[:, k * step : (k + 1) * step, :].reshape(2 * step, width)
        value = jnp.dot(chunk, pick[...], preferred_element_type=jnp.float32).astype(jnp.bfloat16)
        held[0, :, pl.ds(pl.multiple_of(pa * panel + k * step, step), step), :] = value.reshape(2, step, width)

    xcopy, ycopy = {}, {}

    def send_both(k):
        xcopy[k] = send(part(0, k), part(1, k), xs.at[k], xr.at[k], xpeer)
        ycopy[k] = send(part(0, k), part(2, k), ys.at[k], yr.at[k], ypeer)

    permute(0)
    permute(1)
    pl.semaphore_wait(barrier, 4)
    for k in range(2, CHUNKS):
        send_both(k - 2)
        permute(k)
    send_both(CHUNKS - 2)
    send_both(CHUNKS - 1)
    own = held.at[0, :, pl.ds(pl.multiple_of(pa * panel, panel), panel), :]
    shared = [send(own, own, ps.at[0, 0], pr.at[0, 0], cpeer)]
    small = []
    for n, peer in ((1, xpeer), (2, ypeer), (3, dpeer)):
        small.append(send(trace_ref, trace_all.at[n], ss.at[n], sr.at[n], peer))

    def share(rel, k):
        shared.append(send(part(rel, k), part(rel, k), ps.at[rel, k], pr.at[rel, k], cpeer))

    for k in range(CHUNKS):
        xcopy[k].wait_recv()
        share(1, k)
        ycopy[k].wait_recv()
        share(2, k)
    load_trace.wait()
    for copy in small + shared:
        copy.wait_recv()

    pair, base = gx // 2, gy - vert
    right2 = order_y_ref[gy // 2, pair]
    left2 = 1 - right2
    bit_left = order_x_ref[base + left2, pair]
    bit_right = order_x_ref[base + right2, pair]

    def slot(h, v):
        return (h + half) % 2 + 2 * ((v + vert) % 2)

    slots = [
        slot(1 - bit_left, left2), slot(bit_left, left2),
        slot(1 - bit_right, right2), slot(bit_right, right2),
    ]
    here = [jnp.minimum(which, 2) for which in slots]
    first = pl.multiple_of(pa * panel + half * (2 * rows) + vert * rows, rows)

    def times(src, dst, which, use=None, after=None):
        left = src[...].reshape(2 * rows, width)
        for n in range(width // TILE):
            cols = slice(n * TILE, (n + 1) * TILE)
            by = [jnp.dot(left, held[which, c, :, cols], preferred_element_type=jnp.float32) for c in range(2)]
            real = (by[0][:rows] - by[1][rows:]).astype(jnp.bfloat16)
            imag = (by[1][:rows] + by[0][rows:]).astype(jnp.bfloat16)
            if use is not None:
                real = jnp.where(use, real, src[0, :, cols])
                imag = jnp.where(use, imag, src[1, :, cols])
            dst[0, :, cols] = real
            dst[1, :, cols] = imag
            if after is not None and n:
                after(n - 1)
        if after is not None:
            after(width // TILE - 1)

    spot = lax.broadcasted_iota(jnp.int32, (rows, width), 0) + first
    unit = (lax.broadcasted_iota(jnp.int32, (rows, width), 1) == spot).astype(jnp.float32).astype(jnp.bfloat16)
    away = slots[0] == 3
    work[0, 0] = jnp.where(away, unit, held[here[0], 0, pl.ds(first, rows), :])
    work[0, 1] = jnp.where(away, jnp.zeros_like(unit), held[here[0], 1, pl.ds(first, rows), :])
    times(work.at[0], work.at[1], here[1], slots[2] // 3 + slots[3] // 3 > 0)
    peer = {"gx": gx + (1 - 2 * half) * (1 - pa), "gy": gy + (1 - 2 * vert) * pa}
    tiles = width // TILE

    def tile_of(ref, n):
        return ref.at[:, :, n * TILE : (n + 1) * TILE]

    def sender(src, dst, row, copies):
        def after(n):
            copies.append(send(tile_of(src, n), tile_of(dst, n), ts.at[row, n], tr.at[row, n], peer))
        return after

    def times_arriving(copies, src, dst, which, use=None, after=None):
        for n in range(tiles):
            deep = slice(n * TILE, (n + 1) * TILE)
            copies[n].wait_recv()
            left = src[:, :, deep].reshape(2 * rows, TILE)
            for m in range(tiles):
                cols = slice(m * TILE, (m + 1) * TILE)
                by = []
                for c in range(2):
                    term = jnp.dot(left, held[which, c, deep, cols], preferred_element_type=jnp.float32)
                    if n:
                        term += total[c, :, cols]
                    if n < tiles - 1:
                        total[c, :, cols] = term
                    by.append(term)
                if n == tiles - 1:
                    real = (by[0][:rows] - by[1][rows:]).astype(jnp.bfloat16)
                    imag = (by[1][:rows] + by[0][rows:]).astype(jnp.bfloat16)
                    if use is not None:
                        real = jnp.where(use, real, src[0, :, cols])
                        imag = jnp.where(use, imag, src[1, :, cols])
                    dst[0, :, cols] = real
                    dst[1, :, cols] = imag
                    if after is not None and m:
                        after(m - 1)
        if after is not None:
            after(tiles - 1)

    asked, replied = [], []
    times(work.at[1], ask, here[2], slots[3] == 3, sender(ask, ask_in, 0, asked))
    times_arriving(asked, ask_in, reply, 2 - pa, None, sender(reply, reply_in, 1, replied))
    times_arriving(replied, reply_in, work.at[0], here[1], away)
    times(work.at[0], work.at[1], here[2], slots[0] // 3 + slots[1] // 3 > 0)
    times(work.at[1], map_ref, here[3], slots[3] != 3)
    trace = (trace_all[0] + trace_all[1]) + (trace_all[2] + trace_all[3])
    wide = map_ref[...].reshape(2 * rows, width).astype(jnp.float32)
    ones = jnp.ones((8, 128), jnp.float32)
    dims = (((1,), (1,)), ((), ()))
    sums = []
    for c in range(2):
        scaled = wide * trace[c : c + 1]
        folded = scaled[:, :128]
        for n in range(1, width // 128):
            folded += scaled[:, n * 128 : (n + 1) * 128]
        sums.append(lax.dot_general(ones, folded, dims, precision=lax.Precision.HIGHEST, preferred_element_type=jnp.float32))
    out_ref[0:1] = sums[0][0:1, :rows] - sums[1][0:1, rows:]
    out_ref[1:2] = sums[1][0:1, :rows] + sums[0][0:1, rows:]

    for copy in small + list(xcopy.values()) + list(ycopy.values()) + shared + asked + replied:
        copy.wait_send()


def per_device(leaf_maps, face_index, order_x, order_y, traces):
    leaf = leaf_maps[0, 0]
    _, panel, width = leaf.shape
    rows = panel // 4
    vmem = pl.BlockSpec(memory_space=pltpu.VMEM)
    smem = pl.BlockSpec(memory_space=pltpu.SMEM)
    hbm = pl.BlockSpec(memory_space=pl.ANY)
    dma = pltpu.SemaphoreType.DMA
    merged, outgoing = pl.pallas_call(
        kernel,
        out_shape=(
            jax.ShapeDtypeStruct((2, rows, width), jnp.bfloat16),
            jax.ShapeDtypeStruct((2, rows), jnp.float32),
        ),
        in_specs=[smem, smem, hbm, hbm, hbm],
        out_specs=(vmem, vmem),
        scratch_shapes=[
            pltpu.VMEM((3, 2, 2 * panel, width), jnp.bfloat16),
            pltpu.VMEM((2, panel, width), jnp.bfloat16),
            pltpu.VMEM((1, width), jnp.int32),
            pltpu.VMEM((width, width), jnp.bfloat16),
            pltpu.VMEM((4, 2, width), jnp.float32),
            pltpu.VMEM((2, 2, rows, width), jnp.bfloat16),
            pltpu.VMEM((2, rows, width), jnp.bfloat16),
            pltpu.VMEM((2, rows, width), jnp.bfloat16),
            pltpu.VMEM((2, rows, width), jnp.bfloat16),
            pltpu.VMEM((2, rows, width), jnp.bfloat16),
            pltpu.VMEM((2, 2 * rows, width), jnp.float32),
            dma((3,)),
            dma((CHUNKS,)), dma((CHUNKS,)),
            dma((CHUNKS,)), dma((CHUNKS,)),
            dma((3, CHUNKS)), dma((3, CHUNKS)),
            dma((4,)), dma((4,)),
            dma((2, width // TILE)), dma((2, width // TILE)),
        ],
        compiler_params=pltpu.CompilerParams(
            collective_id=0, has_side_effects=True, vmem_limit_bytes=67043328
        ),
    )(order_x.T, order_y.T, leaf, face_index[0], traces[0, 0])
    return (
        merged.reshape(1, 1, 1, 2, rows, width),
        outgoing.reshape(1, 1, 1, 2, rows),
    )


def solution(mesh):
    placed = (
        P("gx", "gy", None, "pa", None),
        P("gx", "gy", None),
        P(),
        P(),
        P("gx", "gy", None, None),
    )
    return jax.shard_map(
        per_device,
        mesh=mesh,
        in_specs=placed,
        out_specs=(P("gx", "gy", "pa", None, None, None), P("gx", "gy", "pa", None, None)),
        check_vma=False,
    )
```

```python
import jax
import jax.numpy as jnp
from jax import lax
from jax.experimental import pallas as pl
from jax.experimental.pallas import tpu as pltpu
from jax.sharding import PartitionSpec as P

MESH = pl.DeviceIdType.MESH
CHUNKS = 8
TILE = 256


def kernel(
    order_x_ref, order_y_ref, leaf_ref, index_ref, trace_ref, map_ref, out_ref,
    held, raw, index_own, pick, trace_all, work, ask, ask_in, reply, reply_in,
    total, local_sem,
    xs, xr, ys, yr, ps, pr, ss, sr, ts, tr,
):
    gx, gy, pa = lax.axis_index("gx"), lax.axis_index("gy"), lax.axis_index("pa")
    half, vert = gx % 2, gy % 2
    xpeer = {"gx": gx + 1 - 2 * half}
    ypeer = {"gy": gy + 1 - 2 * vert}
    dpeer = {"gx": gx + 1 - 2 * half, "gy": gy + 1 - 2 * vert}
    cpeer = {"pa": 1 - pa}
    panel, width = leaf_ref.shape[1], leaf_ref.shape[2]
    step = panel // CHUNKS
    rows = map_ref.shape[1]

    barrier = pltpu.get_barrier_semaphore()
    for peer in (xpeer, ypeer, dpeer, cpeer):
        pl.semaphore_signal(barrier, inc=1, device_id=peer, device_id_type=MESH)

    load_index = pltpu.make_async_copy(index_ref, index_own, local_sem.at[0])
    load_index.start()
    load_leaf = pltpu.make_async_copy(leaf_ref, raw, local_sem.at[1])
    load_leaf.start()
    load_trace = pltpu.make_async_copy(trace_ref, trace_all.at[0], local_sem.at[2])
    load_trace.start()

    def send(src, dst, ssem, rsem, peer):
        copy = pltpu.make_async_remote_copy(
            src_ref=src, dst_ref=dst, send_sem=ssem, recv_sem=rsem,
            device_id=peer, device_id_type=MESH,
        )
        copy.start()
        return copy

    def part(rel, k):
        return held.at[rel, :, pl.ds(pl.multiple_of(pa * panel + k * step, step), step), :]

    load_index.wait()
    index_row = index_own[...]
    grain = 256
    for n in range(width // grain):
        places = lax.broadcasted_iota(jnp.int32, (grain, width), 0) + n * grain
        pick[n * grain : (n + 1) * grain] = (places == index_row).astype(jnp.float32).astype(jnp.bfloat16)
    load_leaf.wait()

    def permute(k):
        chunk = raw[:, k * step : (k + 1) * step, :].reshape(2 * step, width)
        value = jnp.dot(chunk, pick[...], preferred_element_type=jnp.float32).astype(jnp.bfloat16)
        held[0, :, pl.ds(pl.multiple_of(pa * panel + k * step, step), step), :] = value.reshape(2, step, width)

    xcopy, ycopy = {}, {}

    def send_both(k):
        xcopy[k] = send(part(0, k), part(1, k), xs.at[k], xr.at[k], xpeer)
        ycopy[k] = send(part(0, k), part(2, k), ys.at[k], yr.at[k], ypeer)

    permute(0)
    permute(1)
    pl.semaphore_wait(barrier, 4)
    for k in range(2, CHUNKS):
        send_both(k - 2)
        permute(k)
    send_both(CHUNKS - 2)
    send_both(CHUNKS - 1)
    own = held.at[0, :, pl.ds(pl.multiple_of(pa * panel, panel), panel), :]
    shared = [send(own, own, ps.at[0, 0], pr.at[0, 0], cpeer)]
    small = []
    for n, peer in ((1, xpeer), (2, ypeer), (3, dpeer)):
        small.append(send(trace_ref, trace_all.at[n], ss.at[n], sr.at[n], peer))

    def share(rel, k):
        shared.append(send(part(rel, k), part(rel, k), ps.at[rel, k], pr.at[rel, k], cpeer))

    for k in range(CHUNKS):
        xcopy[k].wait_recv()
        share(1, k)
        ycopy[k].wait_recv()
        share(2, k)
    load_trace.wait()
    for copy in small + shared:
        copy.wait_recv()

    pair, base = gx // 2, gy - vert
    right2 = order_y_ref[gy // 2, pair]
    left2 = 1 - right2
    bit_left = order_x_ref[base + left2, pair]
    bit_right = order_x_ref[base + right2, pair]

    def slot(h, v):
        return (h + half) % 2 + 2 * ((v + vert) % 2)

    slots = [
        slot(1 - bit_left, left2), slot(bit_left, left2),
        slot(1 - bit_right, right2), slot(bit_right, right2),
    ]
    here = [jnp.minimum(which, 2) for which in slots]
    first = pl.multiple_of(pa * panel + half * (2 * rows) + vert * rows, rows)

    def times(src, dst, which, use=None, after=None):
        left = src[...].reshape(2 * rows, width)
        for n in range(width // TILE):
            cols = slice(n * TILE, (n + 1) * TILE)
            by = [jnp.dot(left, held[which, c, :, cols], preferred_element_type=jnp.float32) for c in range(2)]
            real = (by[0][:rows] - by[1][rows:]).astype(jnp.bfloat16)
            imag = (by[1][:rows] + by[0][rows:]).astype(jnp.bfloat16)
            if use is not None:
                real = jnp.where(use, real, src[0, :, cols])
                imag = jnp.where(use, imag, src[1, :, cols])
            dst[0, :, cols] = real
            dst[1, :, cols] = imag
            if after is not None and n:
                after(n - 1)
        if after is not None:
            after(width // TILE - 1)

    spot = lax.broadcasted_iota(jnp.int32, (rows, width), 0) + first
    unit = (lax.broadcasted_iota(jnp.int32, (rows, width), 1) == spot).astype(jnp.float32).astype(jnp.bfloat16)
    away = slots[0] == 3
    work[0, 0] = jnp.where(away, unit, held[here[0], 0, pl.ds(first, rows), :])
    work[0, 1] = jnp.where(away, jnp.zeros_like(unit), held[here[0], 1, pl.ds(first, rows), :])
    times(work.at[0], work.at[1], here[1], slots[2] // 3 + slots[3] // 3 > 0)
    peer = {"gx": gx + (1 - 2 * half) * (1 - pa), "gy": gy + (1 - 2 * vert) * pa}
    tiles = width // TILE

    def tile_of(ref, n):
        return ref.at[:, :, n * TILE : (n + 1) * TILE]

    def sender(src, dst, row, copies):
        def after(n):
            copies.append(send(tile_of(src, n), tile_of(dst, n), ts.at[row, n], tr.at[row, n], peer))
        return after

    def times_arriving(copies, src, dst, which, use=None, after=None):
        for n in range(tiles):
            deep = slice(n * TILE, (n + 1) * TILE)
            copies[n].wait_recv()
            left = src[:, :, deep].reshape(2 * rows, TILE)
            for m in range(tiles):
                cols = slice(m * TILE, (m + 1) * TILE)
                by = []
                for c in range(2):
                    term = jnp.dot(left, held[which, c, deep, cols], preferred_element_type=jnp.float32)
                    if n:
                        term += total[c, :, cols]
                    if n < tiles - 1:
                        total[c, :, cols] = term
                    by.append(term)
                if n == tiles - 1:
                    real = (by[0][:rows] - by[1][rows:]).astype(jnp.bfloat16)
                    imag = (by[1][:rows] + by[0][rows:]).astype(jnp.bfloat16)
                    if use is not None:
                        real = jnp.where(use, real, src[0, :, cols])
                        imag = jnp.where(use, imag, src[1, :, cols])
                    dst[0, :, cols] = real
                    dst[1, :, cols] = imag
                    if after is not None and m:
                        after(m - 1)
        if after is not None:
            after(tiles - 1)

    asked, replied = [], []
    times(work.at[1], ask, here[2], slots[3] == 3, sender(ask, ask_in, 0, asked))
    times_arriving(asked, ask_in, reply, 2 - pa, None, sender(reply, reply_in, 1, replied))
    times_arriving(replied, reply_in, work.at[0], here[1], away)
    times(work.at[0], work.at[1], here[2], slots[0] // 3 + slots[1] // 3 > 0)
    times(work.at[1], map_ref, here[3], slots[3] != 3)
    trace = (trace_all[0] + trace_all[1]) + (trace_all[2] + trace_all[3])
    wide = map_ref[...].reshape(2 * rows, width).astype(jnp.float32)
    ones = jnp.ones((8, 128), jnp.float32)
    dims = (((1,), (1,)), ((), ()))
    sums = []
    for c in range(2):
        scaled = wide * trace[c : c + 1]
        folded = scaled[:, :128]
        for n in range(1, width // 128):
            folded += scaled[:, n * 128 : (n + 1) * 128]
        sums.append(lax.dot_general(ones, folded, dims, precision=lax.Precision.HIGHEST, preferred_element_type=jnp.float32))
    out_ref[0:1] = sums[0][0:1, :rows] - sums[1][0:1, rows:]
    out_ref[1:2] = sums[1][0:1, :rows] + sums[0][0:1, rows:]

    for copy in small + list(xcopy.values()) + list(ycopy.values()) + shared + asked + replied:
        copy.wait_send()


def per_device(leaf_maps, face_index, order_x, order_y, traces):
    leaf = leaf_maps[0, 0]
    _, panel, width = leaf.shape
    rows = panel // 4
    vmem = pl.BlockSpec(memory_space=pltpu.VMEM)
    smem = pl.BlockSpec(memory_space=pltpu.SMEM)
    hbm = pl.BlockSpec(memory_space=pl.ANY)
    dma = pltpu.SemaphoreType.DMA
    merged, outgoing = pl.pallas_call(
        kernel,
        out_shape=(
            pltpu.VMEM((2, rows, width), jnp.bfloat16),
            pltpu.VMEM((2, rows), jnp.float32),
        ),
        in_specs=[smem, smem, hbm, hbm, hbm],
        out_specs=(vmem, vmem),
        scratch_shapes=[
            pltpu.VMEM((3, 2, 2 * panel, width), jnp.bfloat16),
            pltpu.VMEM((2, panel, width), jnp.bfloat16),
            pltpu.VMEM((1, width), jnp.int32),
            pltpu.VMEM((width, width), jnp.bfloat16),
            pltpu.VMEM((4, 2, width), jnp.float32),
            pltpu.VMEM((2, 2, rows, width), jnp.bfloat16),
            pltpu.VMEM((2, rows, width), jnp.bfloat16),
            pltpu.VMEM((2, rows, width), jnp.bfloat16),
            pltpu.VMEM((2, rows, width), jnp.bfloat16),
            pltpu.VMEM((2, rows, width), jnp.bfloat16),
            pltpu.VMEM((2, 2 * rows, width), jnp.float32),
            dma((3,)),
            dma((CHUNKS,)), dma((CHUNKS,)),
            dma((CHUNKS,)), dma((CHUNKS,)),
            dma((3, CHUNKS)), dma((3, CHUNKS)),
            dma((4,)), dma((4,)),
            dma((2, width // TILE)), dma((2, width // TILE)),
        ],
        compiler_params=pltpu.CompilerParams(
            collective_id=0, has_side_effects=True, vmem_limit_bytes=60 * 1024 * 1024
        ),
    )(order_x.T, order_y.T, leaf, face_index[0], traces[0, 0])
    return (
        merged.reshape(1, 1, 1, 2, rows, width),
        outgoing.reshape(1, 1, 1, 2, rows),
    )


def solution(mesh):
    placed = (
        P("gx", "gy", None, "pa", None),
        P("gx", "gy", None),
        P(),
        P(),
        P("gx", "gy", None, None),
    )
    return jax.shard_map(
        per_device,
        mesh=mesh,
        in_specs=placed,
        out_specs=(P("gx", "gy", "pa", None, None, None), P("gx", "gy", "pa", None, None)),
        check_vma=False,
    )
```
